32 devices in a mesh: dp: 8 (over z, y), mp: 4 (over x, core).
Axes of the slice: x: 2, y: 2, z: 4, core: 2. Of those that a mesh axis runs over, the one named last changes fastest.
Arguments:
- acts: bfloat16 [8192, 2048], P('dp', 'mp'), may hold values from -6 to 6
- out_grads: bfloat16 [2, 28672, 2048], P(None, 'dp', 'mp'), may hold values from -0.125 to 0.125
- proj_old: float32 [2, 8192, 256], P(None, 'dp'), may hold values from -0.0625 to 0.0625
- moment_one: float32 [2, 28672, 256], P(None, 'dp', 'mp'), may hold values from -12 to 12
- moment_two: float32 [2, 28672, 256], P(None, 'dp', 'mp'), may hold values from 1 to 20
Outputs:
- proj_new: float32 [2, 8192, 256], P(None, 'dp')
- first_new: float32 [2, 28672, 256], P(None, 'dp', 'mp')
- second_new: float32 [2, 28672, 256], P(None, 'dp', 'mp')
- step_update: float32 [2, 28672, 256], P(None, 'dp', 'mp')
The draws below stay inside these ranges and needn't reach their ends.
All inputs are finite; a program needn't handle non-finite values.
Results may differ from the reference program's by a relative error of at most 0.03.
Values may be sent and summed in bfloat16 or wider, within the bound.
A program may use at most 128 MiB of HBM per device.

```python
import math
import jax
import jax.numpy as jnp
from jax import lax

D = 8192
FF = 28672
RANK = 256
SWEEPS = 2
TOKENS = 2048


def block_levels(own_key, shape, pieces, low, largest):
    factor_of, own = 1.0, jax.random.fold_in(own_key, 6)
    for dim, parts in pieces:
        steps = jnp.exp(jax.random.uniform(jax.random.fold_in(own, dim), (parts,), jnp.float32, low / len(pieces), largest / len(pieces)))
        factor_of = factor_of * jnp.repeat(steps, shape[dim] // parts).reshape([-1 if axis == dim else 1 for axis in range(len(shape))])
    return factor_of


def noise(own_key, extent, spread, limit, cuts=(), held_as=jnp.bfloat16):
    values = spread * jax.random.normal(own_key, extent, jnp.float32)
    if cuts:
        values = values * block_levels(own_key, extent, cuts, -0.22, 0.18)
    return jnp.clip(values, -limit, limit).astype(held_as)


def setup_inputs(seed: int = 0) -> dict:
    key_of = jax.random.split(jax.random.key(seed), 6)
    acts = noise(key_of[0], (D, TOKENS), 1.0, 6.0, ((0, 8), (1, 4)))
    out_grads = noise(key_of[1], (2, FF, TOKENS), TOKENS ** -0.5, 0.125, ((1, 8), (2, 4)))
    proj_old = noise(key_of[2], (2, D, RANK), D ** -0.5, 0.0625, ((1, 8),), jnp.float32)
    moment_one = noise(key_of[3], (2, FF, RANK), 2.0, 12.0, ((1, 8), (2, 4)), jnp.float32)
    moment_two = jnp.clip(jnp.exp(math.log(20.0) - 2.9957323 * jax.random.uniform(key_of[4], (2, FF, RANK), jnp.float32) ** block_levels(key_of[4], (2, FF, RANK), ((1, 8), (2, 4)), -0.2, 0.2)), 1.0, 20.0)
    return {"acts": acts, "out_grads": out_grads, "proj_old": proj_old, "moment_one": moment_one, "moment_two": moment_two}


def coefficients(acts32, basis):
    half = basis.astype(jnp.bfloat16).astype(jnp.float32)
    coeff = jnp.einsum('dt,kdr->tkr', acts32, half, precision=lax.Precision.HIGHEST)
    return coeff.astype(jnp.bfloat16).astype(jnp.float32)

def reference(acts, out_grads, proj_old, moment_one, moment_two):
    acts32 = acts.astype(jnp.float32)
    grads32 = out_grads.astype(jnp.float32)
    basis = proj_old
    for sweep in range(SWEEPS):
        coeff = coefficients(acts32, basis)
        hidden = jnp.einsum('kft,tkr->kfr', grads32, coeff, precision=lax.Precision.HIGHEST)
        hidden = hidden.astype(jnp.bfloat16).astype(jnp.float32)
        token_image = jnp.einsum('kft,kfr->tkr', grads32, hidden, precision=lax.Precision.HIGHEST)
        token_image = token_image.astype(jnp.bfloat16).astype(jnp.float32)
        image = jnp.einsum('dt,tkr->kdr', acts32, token_image, precision=lax.Precision.HIGHEST)
        gram = jnp.einsum('kdr,kds->krs', image, image, precision=lax.Precision.HIGHEST)
        lower = jnp.linalg.cholesky(gram)
        solved = jax.scipy.linalg.solve_triangular(lower, jnp.swapaxes(image, 1, 2), lower=True)
        basis = jnp.swapaxes(solved, 1, 2)
    coeff = coefficients(acts32, basis)
    projected = jnp.einsum('kft,tkr->kfr', grads32, coeff, precision=lax.Precision.HIGHEST)
    first_new = 0.9 * moment_one + 0.1 * projected
    second_new = 0.999 * moment_two + 0.001 * projected * projected
    step_update = first_new / (jnp.sqrt(second_new) + 1e-08)
    return (basis, first_new, second_new, step_update)
```

```python
import functools

import jax
import jax.numpy as jnp
from jax import lax
from jax.experimental import pallas as pl
from jax.experimental.pallas import tpu as pltpu
from jax.sharding import PartitionSpec as P

SWEEPS = 2
BLOCK = 32
VMEM_LIMIT = 48 << 20


def greet(peers):
    barrier = pltpu.get_barrier_semaphore()
    for peer in peers:
        pl.semaphore_signal(barrier, inc=1, device_id=peer, device_id_type=pl.DeviceIdType.MESH)
    pl.semaphore_wait(barrier, len(peers))


def remote(src, dst, send_sem, recv_sem, peer):
    return pltpu.make_async_remote_copy(
        src_ref=src,
        dst_ref=dst,
        send_sem=send_sem,
        recv_sem=recv_sem,
        device_id=peer,
        device_id_type=pl.DeviceIdType.MESH,
    )


def reduce_dp_kernel(n, x_ref, out_ref, got, send_a, recv_a, send_b, recv_b):
    me = lax.axis_index("dp")
    peers = [lax.rem(me + step, n) for step in range(1, n)]
    greet([{"dp": peer} for peer in peers])
    first = []
    for i, peer in enumerate(peers):
        copy = remote(x_ref.at[peer], got.at[i], send_a.at[i], recv_a.at[i], {"dp": peer})
        copy.start()
        first.append(copy)
    total = x_ref[me].astype(jnp.float32)
    for i, copy in enumerate(first):
        copy.wait_recv()
        total = total + got[i].astype(jnp.float32)
    out_ref[me] = total.astype(out_ref.dtype)
    second = []
    for i, peer in enumerate(peers):
        copy = remote(out_ref.at[me], out_ref.at[me], send_b.at[i], recv_b.at[i], {"dp": peer})
        copy.start()
        second.append(copy)
    for i, copy in enumerate(second):
        source = lax.rem(me + n - 1 - i, n)
        landed = out_ref.at[source]
        remote(landed, landed, send_b.at[i], recv_b.at[i], {"dp": peers[i]}).wait_recv()
    for copy in first + second:
        copy.wait_send()


def reduce_dp(n, x, collective_id):
    rows, columns = x.shape
    piece = rows // n
    out = pl.pallas_call(
        functools.partial(reduce_dp_kernel, n),
        out_shape=jax.ShapeDtypeStruct((n, piece, columns), x.dtype),
        in_specs=[pl.BlockSpec(memory_space=pltpu.VMEM)],
        out_specs=pl.BlockSpec(memory_space=pltpu.VMEM),
        scratch_shapes=[pltpu.VMEM((n - 1, piece, columns), x.dtype)]
        + [pltpu.SemaphoreType.DMA((n - 1,))] * 4,
        compiler_params=pltpu.CompilerParams(
            collective_id=collective_id, has_side_effects=True, vmem_limit_bytes=VMEM_LIMIT
        ),
        name="reduce_dp",
    )(x.reshape(n, piece, columns))
    return out.reshape(rows, columns)


def reduce_mp_kernel(chunks, scatter, x_ref, out_ref, got_a, mid, got_b, sems):
    me = lax.axis_index("mp")
    low, high = lax.rem(me, 2), me // 2
    mate = {"mp": high * 2 + 1 - low}
    across = {"mp": (1 - high) * 2 + low}
    rows = x_ref.shape[1]
    piece = rows // chunks
    width = out_ref.shape[2]
    mine = pl.ds(pl.multiple_of(high * width, 128), width) if scatter else slice(None)
    theirs = pl.ds(pl.multiple_of((1 - high) * width, 128), width) if scatter else slice(None)
    greet([mate, across])
    stage_a, stage_b, stage_c = [], [], []
    for c in range(chunks):
        span = pl.ds(c * piece, piece)
        copy = remote(
            x_ref.at[1 - low, span], got_a.at[span], sems.at[0, c], sems.at[1, c], mate
        )
        copy.start()
        stage_a.append(copy)
    for c in range(chunks):
        span = pl.ds(c * piece, piece)
        stage_a[c].wait_recv()
        mid[span] = (
            x_ref[low, span].astype(jnp.float32) + got_a[span].astype(jnp.float32)
        ).astype(mid.dtype)
        copy = remote(mid.at[span, theirs], got_b.at[span], sems.at[2, c], sems.at[3, c], across)
        copy.start()
        stage_b.append(copy)
    for c in range(chunks):
        span = pl.ds(c * piece, piece)
        stage_b[c].wait_recv()
        out_ref[low, span] = (
            mid[span, mine].astype(jnp.float32) + got_b[span].astype(jnp.float32)
        ).astype(out_ref.dtype)
        copy = remote(
            out_ref.at[low, span], out_ref.at[low, span], sems.at[4, c], sems.at[5, c], mate
        )
        copy.start()
        stage_c.append(copy)
    for c in range(chunks):
        landed = out_ref.at[1 - low, pl.ds(c * piece, piece)]
        remote(landed, landed, sems.at[4, c], sems.at[5, c], mate).wait_recv()
    for copy in stage_a + stage_b + stage_c:
        copy.wait_send()


def reduce_mp(x, chunks, scatter, collective_id):
    rows, columns = x.shape
    half = rows // 2
    width = columns // 2 if scatter else columns
    out = pl.pallas_call(
        functools.partial(reduce_mp_kernel, chunks, scatter),
        out_shape=jax.ShapeDtypeStruct((2, half, width), x.dtype),
        in_specs=[pl.BlockSpec(memory_space=pltpu.VMEM)],
        out_specs=pl.BlockSpec(memory_space=pltpu.VMEM),
        scratch_shapes=[
            pltpu.VMEM((half, columns), x.dtype),
            pltpu.VMEM((half, columns), x.dtype),
            pltpu.VMEM((half, width), x.dtype),
            pltpu.SemaphoreType.DMA((6, chunks)),
        ],
        compiler_params=pltpu.CompilerParams(
            collective_id=collective_id, has_side_effects=True, vmem_limit_bytes=VMEM_LIMIT
        ),
        name="reduce_mp",
    )(x.reshape(2, half, columns))
    return out.reshape(rows, width)


def inverse_factor_kernel(gram_ref, out_ref, work):
    parts, size, _ = gram_ref.shape
    exact = functools.partial(
        lax.dot_general, precision=lax.Precision.HIGHEST, preferred_element_type=jnp.float32
    )
    row = lax.broadcasted_iota(jnp.int32, (size, size), 0)
    column = lax.broadcasted_iota(jnp.int32, (size, size), 1)
    for k in range(parts):
        work[k, :, :size] = gram_ref[k]
        work[k, :, size:] = jnp.where(row == column, 1.0, 0.0)
    small_row = lax.broadcasted_iota(jnp.int32, (BLOCK, 2 * BLOCK), 0)
    small_column = lax.broadcasted_iota(jnp.int32, (BLOCK, 2 * BLOCK), 1)
    for start in range(0, size, BLOCK):
        stop = start + BLOCK
        blocks = []
        for k in range(parts):
            corner = work[k, start:stop, start:stop]
            blocks.append(
                jnp.concatenate(
                    [corner, jnp.where(small_row == small_column, 1.0, 0.0)[:, :BLOCK]], axis=1
                )
            )
        scales = [jnp.zeros((BLOCK, 1), jnp.float32) for _ in range(parts)]
        index = lax.broadcasted_iota(jnp.int32, (BLOCK, 1), 0)
        for j in range(BLOCK):
            for k in range(parts):
                block = blocks[k]
                pivot = block[j : j + 1, j : j + 1]
                scales[k] = jnp.where(index == j, lax.rsqrt(pivot), scales[k])
                factor = jnp.where(index > j, block[:, j : j + 1], 0.0)
                blocks[k] = block - factor * (block[j : j + 1, :] * (1.0 / pivot))
        for k in range(parts):
            inverse = blocks[k][:, BLOCK:] * scales[k]
            done = exact(inverse, work[k, start:stop, :], (((1,), (0,)), ((), ())))
            out_ref[k, start:stop, :] = done[:, size:]
            if stop < size:
                below = exact(work[k, stop:, start:stop], inverse, (((1,), (1,)), ((), ())))
                work[k, stop:, :] -= exact(below, done, (((1,), (0,)), ((), ())))


def inverse_factor(gram):
    parts, size, _ = gram.shape
    return pl.pallas_call(
        inverse_factor_kernel,
        out_shape=jax.ShapeDtypeStruct(gram.shape, jnp.float32),
        in_specs=[pl.BlockSpec(memory_space=pltpu.VMEM)],
        out_specs=pl.BlockSpec(memory_space=pltpu.VMEM),
        scratch_shapes=[pltpu.VMEM((parts, size, 2 * size), jnp.float32)],
        compiler_params=pltpu.CompilerParams(vmem_limit_bytes=VMEM_LIMIT),
        name="inverse_factor",
    )(gram)


def shards(dp, acts, out_grads, proj_old, moment_one, moment_two):
    half = jnp.bfloat16
    parts, units, tokens = out_grads.shape
    features, rank = proj_old.shape[1:]
    einsum = functools.partial(jnp.einsum, preferred_element_type=jnp.float32)

    def token_product(basis):
        local = einsum("dt,kdr->ktr", acts, basis.astype(half)).astype(half)
        coeff = reduce_dp(dp, local.reshape(parts * tokens, rank), 0)
        product = einsum("kft,ktr->kfr", out_grads, coeff.reshape(parts, tokens, rank))
        return product.astype(half).reshape(parts * units, rank)

    basis = proj_old
    for sweep in range(SWEEPS):
        hidden = reduce_mp(token_product(basis), 7, False, 1).reshape(parts, units, rank)
        token_part = einsum("kft,kfr->ktr", out_grads, hidden).astype(half)
        token_image = reduce_dp(dp, token_part.reshape(parts * tokens, rank), 0)
        image_part = einsum("dt,ktr->kdr", acts, token_image.reshape(parts, tokens, rank))
        image = reduce_mp(image_part.astype(half).reshape(parts * features, rank), 4, False, 2)
        image = image.reshape(parts, features, rank)
        gram_local = einsum("kdr,kds->krs", image, image)
        gram = reduce_dp(dp, gram_local.reshape(parts * rank, rank), 3)
        inverse = inverse_factor(gram.reshape(parts, rank, rank))
        basis = jnp.einsum(
            "kdr,ksr->kds",
            image.astype(jnp.float32),
            inverse,
            precision=lax.Precision.HIGHEST,
        )
    projected = reduce_mp(token_product(basis), 7, True, 4)
    share = rank // 4
    low = lax.rem(lax.axis_index("mp"), 2)
    projected = lax.dynamic_slice_in_dim(projected, low * share, share, 1)
    projected = projected.reshape(parts, units, share).astype(jnp.float32)
    first_new = 0.9 * moment_one + 0.1 * projected
    second_new = 0.999 * moment_two + 0.001 * projected * projected
    step_update = first_new / (jnp.sqrt(second_new) + 1e-08)
    return (basis, first_new, second_new, step_update)


def solution(mesh):
    assert mesh.shape["mp"] == 4
    placed = (
        P("dp", "mp"),
        P(None, "dp", "mp"),
        P(None, "dp", None),
        P(None, "dp", "mp"),
        P(None, "dp", "mp"),
    )
    return jax.shard_map(
        functools.partial(shards, mesh.shape["dp"]),
        mesh=mesh,
        in_specs=placed,
        out_specs=(
            P(None, "dp", None),
            P(None, "dp", "mp"),
            P(None, "dp", "mp"),
            P(None, "dp", "mp"),
        ),
        check_vma=False,
    )
```

```python
import functools

import jax
import jax.numpy as jnp
from jax import lax
from jax.experimental import pallas as pl
from jax.experimental.pallas import tpu as pltpu
from jax.sharding import PartitionSpec as P

SWEEPS = 2
BLOCK = 32
GROUP = 4
VMEM_LIMIT = 48 << 20


def greet(peers):
    barrier = pltpu.get_barrier_semaphore()
    for peer in peers:
        pl.semaphore_signal(barrier, inc=1, device_id=peer, device_id_type=pl.DeviceIdType.MESH)
    pl.semaphore_wait(barrier, len(peers))


def remote(src, dst, send_sem, recv_sem, peer):
    return pltpu.make_async_remote_copy(
        src_ref=src,
        dst_ref=dst,
        send_sem=send_sem,
        recv_sem=recv_sem,
        device_id=peer,
        device_id_type=pl.DeviceIdType.MESH,
    )


def reduce_dp_kernel(n, x_ref, out_ref, got, send_a, recv_a, send_b, recv_b):
    me = lax.axis_index("dp")
    peers = [lax.rem(me + step, n) for step in range(1, n)]
    greet([{"dp": peer} for peer in peers])
    first = []
    for i, peer in enumerate(peers):
        copy = remote(x_ref.at[peer], got.at[i], send_a.at[i], recv_a.at[i], {"dp": peer})
        copy.start()
        first.append(copy)
    total = x_ref[me].astype(jnp.float32)
    for i, copy in enumerate(first):
        copy.wait_recv()
        total = total + got[i].astype(jnp.float32)
    out_ref[me] = total.astype(out_ref.dtype)
    second = []
    for i, peer in enumerate(peers):
        copy = remote(out_ref.at[me], out_ref.at[me], send_b.at[i], recv_b.at[i], {"dp": peer})
        copy.start()
        second.append(copy)
    for i, copy in enumerate(second):
        source = lax.rem(me + n - 1 - i, n)
        landed = out_ref.at[source]
        remote(landed, landed, send_b.at[i], recv_b.at[i], {"dp": peers[i]}).wait_recv()
    for copy in first + second:
        copy.wait_send()


def reduce_dp(n, x, collective_id):
    rows, columns = x.shape
    piece = rows // n
    out = pl.pallas_call(
        functools.partial(reduce_dp_kernel, n),
        out_shape=jax.ShapeDtypeStruct((n, piece, columns), x.dtype),
        in_specs=[pl.BlockSpec(memory_space=pltpu.VMEM)],
        out_specs=pl.BlockSpec(memory_space=pltpu.VMEM),
        scratch_shapes=[pltpu.VMEM((n - 1, piece, columns), x.dtype)]
        + [pltpu.SemaphoreType.DMA((n - 1,))] * 4,
        compiler_params=pltpu.CompilerParams(
            collective_id=collective_id, has_side_effects=True, vmem_limit_bytes=VMEM_LIMIT
        ),
        name="reduce_dp",
    )(x.reshape(n, piece, columns))
    return out.reshape(rows, columns)


def reduce_mp_kernel(chunks, scatter, x_ref, out_ref, got_a, mid, got_b, sems):
    me = lax.axis_index("mp")
    low, high = lax.rem(me, 2), me // 2
    mate = {"mp": high * 2 + 1 - low}
    across = {"mp": (1 - high) * 2 + low}
    rows = x_ref.shape[1]
    piece = rows // chunks
    width = out_ref.shape[2]
    mine = pl.ds(pl.multiple_of(high * width, 128), width) if scatter else slice(None)
    theirs = pl.ds(pl.multiple_of((1 - high) * width, 128), width) if scatter else slice(None)
    greet([mate, across])
    stage_a, stage_b, stage_c = [], [], []
    for c in range(chunks):
        span = pl.ds(c * piece, piece)
        copy = remote(
            x_ref.at[1 - low, span], got_a.at[span], sems.at[0, c], sems.at[1, c], mate
        )
        copy.start()
        stage_a.append(copy)
    for c in range(chunks):
        span = pl.ds(c * piece, piece)
        stage_a[c].wait_recv()
        mid[span] = (
            x_ref[low, span].astype(jnp.float32) + got_a[span].astype(jnp.float32)
        ).astype(mid.dtype)
        copy = remote(mid.at[span, theirs], got_b.at[span], sems.at[2, c], sems.at[3, c], across)
        copy.start()
        stage_b.append(copy)
    for c in range(chunks):
        span = pl.ds(c * piece, piece)
        stage_b[c].wait_recv()
        out_ref[low, span] = (
            mid[span, mine].astype(jnp.float32) + got_b[span].astype(jnp.float32)
        ).astype(out_ref.dtype)
        copy = remote(
            out_ref.at[low, span], out_ref.at[low, span], sems.at[4, c], sems.at[5, c], mate
        )
        copy.start()
        stage_c.append(copy)
    for c in range(chunks):
        landed = out_ref.at[1 - low, pl.ds(c * piece, piece)]
        remote(landed, landed, sems.at[4, c], sems.at[5, c], mate).wait_recv()
    for copy in stage_a + stage_b + stage_c:
        copy.wait_send()


def reduce_mp(x, chunks, scatter, collective_id):
    rows, columns = x.shape
    half = rows // 2
    width = columns // 2 if scatter else columns
    out = pl.pallas_call(
        functools.partial(reduce_mp_kernel, chunks, scatter),
        out_shape=jax.ShapeDtypeStruct((2, half, width), x.dtype),
        in_specs=[pl.BlockSpec(memory_space=pltpu.VMEM)],
        out_specs=pl.BlockSpec(memory_space=pltpu.VMEM),
        scratch_shapes=[
            pltpu.VMEM((half, columns), x.dtype),
            pltpu.VMEM((half, columns), x.dtype),
            pltpu.VMEM((half, width), x.dtype),
            pltpu.SemaphoreType.DMA((6, chunks)),
        ],
        compiler_params=pltpu.CompilerParams(
            collective_id=collective_id, has_side_effects=True, vmem_limit_bytes=VMEM_LIMIT
        ),
        name="reduce_mp",
    )(x.reshape(2, half, columns))
    return out.reshape(rows, width)


def eliminate(blocks):
    shape = (BLOCK // 8, 8, 2 * BLOCK)
    index = lax.broadcasted_iota(jnp.int32, shape, 0) * 8 + lax.broadcasted_iota(
        jnp.int32, shape, 1
    )
    wide = (8, 2 * BLOCK)
    blocks = [block.reshape(shape) for block in blocks]
    scales = [jnp.zeros(shape, jnp.float32) for _ in blocks]
    for j in range(0, BLOCK, GROUP):
        for k, block in enumerate(blocks):
            rows, columns, cross = [], [], []
            for q in range(GROUP):
                line = block[(j + q) // 8, (j + q) % 8 : (j + q) % 8 + 1, :]
                rows.append(jnp.broadcast_to(line, wide))
                columns.append(jnp.broadcast_to(block[:, :, j + q : j + q + 1], shape))
                cross.append(
                    [jnp.broadcast_to(line[:, j + s : j + s + 1], wide) for s in range(GROUP)]
                )
            for q in range(GROUP):
                pivot = cross[q][q]
                reciprocal = 1.0 / pivot
                for s in range(q + 1, GROUP):
                    ratio = cross[q][s] * reciprocal
                    for u in range(s, GROUP):
                        cross[s][u] = cross[s][u] - ratio * cross[q][u]
                    rows[s] = rows[s] - ratio * rows[q]
                    columns[s] = columns[s] - ratio[None] * columns[q]
                factor = jnp.where(index > j + q, columns[q], 0.0)
                block = block - factor * (rows[q] * reciprocal)[None]
                scales[k] = jnp.where(index == j + q, lax.rsqrt(pivot)[None], scales[k])
            blocks[k] = block
    return [
        (block * scale).reshape(BLOCK, 2 * BLOCK)[:, BLOCK:]
        for block, scale in zip(blocks, scales)
    ]


def inverse_factor(out_ref, work):
    parts, size, _ = out_ref.shape
    exact = functools.partial(
        lax.dot_general, precision=lax.Precision.HIGHEST, preferred_element_type=jnp.float32
    )
    row = lax.broadcasted_iota(jnp.int32, (size, size), 0)
    column = lax.broadcasted_iota(jnp.int32, (size, size), 1)
    for k in range(parts):
        work[k, :, size:] = jnp.where(row == column, 1.0, 0.0)
    small = jnp.where(row == column, 1.0, 0.0)[:BLOCK, :BLOCK]
    for start in range(0, size, BLOCK):
        stop = start + BLOCK
        inverses = eliminate(
            [
                jnp.concatenate([work[k, start:stop, start:stop], small], axis=1)
                for k in range(parts)
            ]
        )
        for k, inverse in enumerate(inverses):
            done = exact(inverse, work[k, start:stop, :], (((1,), (0,)), ((), ())))
            out_ref[k, start:stop, :] = done[:, size:]
            if stop < size:
                below = exact(work[k, stop:, start:stop], inverse, (((1,), (1,)), ((), ())))
                work[k, stop:, :] -= exact(below, done, (((1,), (0,)), ((), ())))


def settle_kernel(
    n, gram_ref, local_ref, coeff_ref, inverse_ref, got_g, got_c, full, work, sem_g, sem_c, sem_m
):
    me, quarter = lax.axis_index("dp"), lax.axis_index("mp")
    parts, size, _ = inverse_ref.shape
    peers = [{"dp": lax.rem(me + step, n)} for step in range(1, n)]
    beside = [{"mp": lax.rem(quarter + step, 4)} for step in range(1, 4)]
    greet(peers + beside)
    started = []

    def send(*copy):
        started.append(remote(*copy))
        started[-1].start()

    for i, peer in enumerate(peers):
        send(gram_ref.at[quarter, peer["dp"]], got_g.at[i], sem_g.at[0, i], sem_g.at[1, i], peer)
    for i, peer in enumerate(peers):
        send(local_ref.at[peer["dp"]], got_c.at[i], sem_c.at[0, i], sem_c.at[1, i], peer)
    total = gram_ref[quarter, me]
    for i, peer in enumerate(peers):
        remote(got_g.at[i], got_g.at[i], sem_g.at[0, i], sem_g.at[1, i], peer).wait_recv()
        total = total + got_g[i]
    full[quarter, me] = total
    own = full.at[quarter, me]
    for i, peer in enumerate(peers):
        send(own, own, sem_g.at[2, i], sem_g.at[3, i], peer)
    for i, peer in enumerate(peers):
        landed = full.at[quarter, lax.rem(me + n - 1 - i, n)]
        remote(landed, landed, sem_g.at[2, i], sem_g.at[3, i], peer).wait_recv()
    for i, peer in enumerate(beside):
        send(full.at[quarter], full.at[quarter], sem_m.at[0, i], sem_m.at[1, i], peer)
    for i, peer in enumerate(beside):
        landed = full.at[lax.rem(quarter + 3 - i, 4)]
        remote(landed, landed, sem_m.at[0, i], sem_m.at[1, i], peer).wait_recv()
    for k in range(parts):
        work[k, :, :size] = full[2 * k : 2 * k + 2].reshape(size, size)
    inverse_factor(inverse_ref, work)
    total = local_ref[me]
    for i, peer in enumerate(peers):
        remote(got_c.at[i], got_c.at[i], sem_c.at[0, i], sem_c.at[1, i], peer).wait_recv()
        total = total + got_c[i]
    coeff_ref[me] = lax.dot_general(
        total,
        inverse_ref[me // (n // parts)],
        (((1,), (1,)), ((), ())),
        precision=lax.Precision.HIGHEST,
        preferred_element_type=jnp.float32,
    ).astype(coeff_ref.dtype)
    own = coeff_ref.at[me]
    for i, peer in enumerate(peers):
        send(own, own, sem_c.at[2, i], sem_c.at[3, i], peer)
    for i, peer in enumerate(peers):
        landed = coeff_ref.at[lax.rem(me + n - 1 - i, n)]
        remote(landed, landed, sem_c.at[2, i], sem_c.at[3, i], peer).wait_recv()
    for copy in started:
        copy.wait_send()


def settle(n, gram, local, collective_id):
    parts, size, _ = gram.shape
    rows, columns = local.shape
    piece, share = rows // n, parts * size // (4 * n)
    coeff, inverse = pl.pallas_call(
        functools.partial(settle_kernel, n),
        out_shape=(
            jax.ShapeDtypeStruct((n, piece, columns), jnp.bfloat16),
            jax.ShapeDtypeStruct(gram.shape, jnp.float32),
        ),
        in_specs=[pl.BlockSpec(memory_space=pltpu.VMEM)] * 2,
        out_specs=[pl.BlockSpec(memory_space=pltpu.VMEM)] * 2,
        scratch_shapes=[
            pltpu.VMEM((n - 1, share, size), jnp.float32),
            pltpu.VMEM((n - 1, piece, columns), jnp.float32),
            pltpu.VMEM((4, n, share, size), jnp.float32),
            pltpu.VMEM((parts, size, 2 * size), jnp.float32),
            pltpu.SemaphoreType.DMA((4, n - 1)),
            pltpu.SemaphoreType.DMA((4, n - 1)),
            pltpu.SemaphoreType.DMA((2, 3)),
        ],
        compiler_params=pltpu.CompilerParams(
            collective_id=collective_id, has_side_effects=True, vmem_limit_bytes=VMEM_LIMIT
        ),
        name="settle",
    )(gram.reshape(4, n, share, size), local.reshape(n, piece, columns))
    return coeff.reshape(rows, columns), inverse


def shards(dp, acts, out_grads, proj_old, moment_one, moment_two):
    half = jnp.bfloat16
    parts, units, tokens = out_grads.shape
    features, rank = proj_old.shape[1:]
    einsum = functools.partial(jnp.einsum, preferred_element_type=jnp.float32)

    def feature_product(basis_half):
        return einsum("dt,kdr->ktr", acts, basis_half).reshape(parts * tokens, rank)

    def grads_product(coeff):
        product = einsum("kft,ktr->kfr", out_grads, coeff.reshape(parts, tokens, rank))
        return product.astype(half).reshape(parts * units, rank)

    def sweep(_, carried):
        hidden = reduce_mp(grads_product(carried[0]), 7, False, 1).reshape(parts, units, rank)
        token_part = einsum("kft,kfr->ktr", out_grads, hidden).astype(half)
        token_image = reduce_dp(dp, token_part.reshape(parts * tokens, rank), 0)
        image_part = einsum("dt,ktr->kdr", acts, token_image.reshape(parts, tokens, rank))
        image = reduce_mp(image_part.astype(half).reshape(parts * features, rank), 4, False, 2)
        image = image.reshape(parts, features, rank)
        coeff, inverse = settle(
            dp, einsum("kdr,kds->krs", image, image), feature_product(image), 3
        )
        return coeff, image, inverse

    coeff = reduce_dp(dp, feature_product(proj_old.astype(half)).astype(half), 0)
    empty = jnp.zeros((parts, features, rank), half), jnp.zeros((parts, rank, rank), jnp.float32)
    coeff, image, inverse = lax.fori_loop(0, SWEEPS, sweep, (coeff, *empty))
    basis = jnp.einsum(
        "kdr,ksr->kds", image.astype(jnp.float32), inverse, precision=lax.Precision.HIGHEST
    )
    projected = reduce_mp(grads_product(coeff), 7, True, 4)
    share = rank // 4
    low = lax.rem(lax.axis_index("mp"), 2)
    projected = lax.dynamic_slice_in_dim(projected, low * share, share, 1)
    projected = projected.reshape(parts, units, share).astype(jnp.float32)
    first_new = 0.9 * moment_one + 0.1 * projected
    second_new = 0.999 * moment_two + 0.001 * projected * projected
    step_update = first_new / (jnp.sqrt(second_new) + 1e-08)
    return (basis, first_new, second_new, step_update)


def solution(mesh):
    assert mesh.shape["mp"] == 4
    placed = (
        P("dp", "mp"),
        P(None, "dp", "mp"),
        P(None, "dp", None),
        P(None, "dp", "mp"),
        P(None, "dp", "mp"),
    )
    return jax.shard_map(
        functools.partial(shards, mesh.shape["dp"]),
        mesh=mesh,
        in_specs=placed,
        out_specs=(
            P(None, "dp", None),
            P(None, "dp", "mp"),
            P(None, "dp", "mp"),
            P(None, "dp", "mp"),
        ),
        check_vma=False,
    )
```

```python
import functools

import jax
import jax.numpy as jnp
from jax import lax
from jax.experimental import pallas as pl
from jax.experimental.pallas import tpu as pltpu
from jax.sharding import PartitionSpec as P

SWEEPS = 2
BLOCK = 64
GROUP = 4
VMEM_LIMIT = 48 << 20


def greet(peers):
    barrier = pltpu.get_barrier_semaphore()
    for peer in peers:
        pl.semaphore_signal(barrier, inc=1, device_id=peer, device_id_type=pl.DeviceIdType.MESH)
    pl.semaphore_wait(barrier, len(peers))


def remote(src, dst, send_sem, recv_sem, peer):
    return pltpu.make_async_remote_copy(
        src_ref=src,
        dst_ref=dst,
        send_sem=send_sem,
        recv_sem=recv_sem,
        device_id=peer,
        device_id_type=pl.DeviceIdType.MESH,
    )


def reduce_dp_kernel(n, x_ref, out_ref, got, send_a, recv_a, send_b, recv_b):
    me = lax.axis_index("dp")
    peers = [lax.rem(me + step, n) for step in range(1, n)]
    greet([{"dp": peer} for peer in peers])
    first = []
    for i, peer in enumerate(peers):
        copy = remote(x_ref.at[peer], got.at[i], send_a.at[i], recv_a.at[i], {"dp": peer})
        copy.start()
        first.append(copy)
    total = x_ref[me].astype(jnp.float32)
    for i, copy in enumerate(first):
        copy.wait_recv()
        total = total + got[i].astype(jnp.float32)
    out_ref[me] = total.astype(out_ref.dtype)
    second = []
    for i, peer in enumerate(peers):
        copy = remote(out_ref.at[me], out_ref.at[me], send_b.at[i], recv_b.at[i], {"dp": peer})
        copy.start()
        second.append(copy)
    for i, copy in enumerate(second):
        source = lax.rem(me + n - 1 - i, n)
        landed = out_ref.at[source]
        remote(landed, landed, send_b.at[i], recv_b.at[i], {"dp": peers[i]}).wait_recv()
    for copy in first + second:
        copy.wait_send()


def reduce_dp(n, x, collective_id):
    rows, columns = x.shape
    piece = rows // n
    out = pl.pallas_call(
        functools.partial(reduce_dp_kernel, n),
        out_shape=jax.ShapeDtypeStruct((n, piece, columns), x.dtype),
        in_specs=[pl.BlockSpec(memory_space=pltpu.VMEM)],
        out_specs=pl.BlockSpec(memory_space=pltpu.VMEM),
        scratch_shapes=[pltpu.VMEM((n - 1, piece, columns), x.dtype)]
        + [pltpu.SemaphoreType.DMA((n - 1,))] * 4,
        compiler_params=pltpu.CompilerParams(
            collective_id=collective_id, has_side_effects=True, vmem_limit_bytes=VMEM_LIMIT
        ),
        name="reduce_dp",
    )(x.reshape(n, piece, columns))
    return out.reshape(rows, columns)


def reduce_mp_kernel(chunks, x_ref, out_ref, got_a, mid, got_b, sems):
    me = lax.axis_index("mp")
    low, high = lax.rem(me, 2), me // 2
    mate = {"mp": high * 2 + 1 - low}
    across = {"mp": (1 - high) * 2 + low}
    rows = x_ref.shape[1]
    piece = rows // chunks
    greet([mate, across])
    stage_a, stage_b, stage_c = [], [], []
    for c in range(chunks):
        span = pl.ds(c * piece, piece)
        copy = remote(
            x_ref.at[1 - low, span], got_a.at[span], sems.at[0, c], sems.at[1, c], mate
        )
        copy.start()
        stage_a.append(copy)
    for c in range(chunks):
        span = pl.ds(c * piece, piece)
        stage_a[c].wait_recv()
        mid[span] = (
            x_ref[low, span].astype(jnp.float32) + got_a[span].astype(jnp.float32)
        ).astype(mid.dtype)
        copy = remote(mid.at[span], got_b.at[span], sems.at[2, c], sems.at[3, c], across)
        copy.start()
        stage_b.append(copy)
    for c in range(chunks):
        span = pl.ds(c * piece, piece)
        stage_b[c].wait_recv()
        out_ref[low, span] = (
            mid[span].astype(jnp.float32) + got_b[span].astype(jnp.float32)
        ).astype(out_ref.dtype)
        copy = remote(
            out_ref.at[low, span], out_ref.at[low, span], sems.at[4, c], sems.at[5, c], mate
        )
        copy.start()
        stage_c.append(copy)
    for c in range(chunks):
        landed = out_ref.at[1 - low, pl.ds(c * piece, piece)]
        remote(landed, landed, sems.at[4, c], sems.at[5, c], mate).wait_recv()
    for copy in stage_a + stage_b + stage_c:
        copy.wait_send()


def reduce_mp(x, chunks, collective_id):
    rows, columns = x.shape
    half = rows // 2
    out = pl.pallas_call(
        functools.partial(reduce_mp_kernel, chunks),
        out_shape=jax.ShapeDtypeStruct((2, half, columns), x.dtype),
        in_specs=[pl.BlockSpec(memory_space=pltpu.VMEM)],
        out_specs=pl.BlockSpec(memory_space=pltpu.VMEM),
        scratch_shapes=[
            pltpu.VMEM((half, columns), x.dtype),
            pltpu.VMEM((half, columns), x.dtype),
            pltpu.VMEM((half, columns), x.dtype),
            pltpu.SemaphoreType.DMA((6, chunks)),
        ],
        compiler_params=pltpu.CompilerParams(
            collective_id=collective_id, has_side_effects=True, vmem_limit_bytes=VMEM_LIMIT
        ),
        name="reduce_mp",
    )(x.reshape(2, half, columns))
    return out.reshape(rows, columns)


def hidden_kernel(
    chunks, scatter, grads_ref, coeff_ref, out_ref, grads, sent, own, got_a, mid, got_b, hidden,
    total, load_sem, sems
):
    me = lax.axis_index("mp")
    low, high = lax.rem(me, 2), me // 2
    mate = {"mp": high * 2 + 1 - low}
    across = {"mp": (1 - high) * 2 + low}
    parts, units, tokens = grads_ref.shape
    piece = units // chunks
    result = out_ref if scatter else hidden
    width = result.shape[2]
    mine = pl.ds(pl.multiple_of(high * width, 128), width) if scatter else slice(None)
    theirs = pl.ds(pl.multiple_of((1 - high) * width, 128), width) if scatter else slice(None)

    def span(c):
        return pl.ds(pl.multiple_of(c * piece, piece), piece)

    def load(c, side):
        k = 1 - low if side == 0 else low
        return pltpu.make_async_copy(
            grads_ref.at[k, span(c)], grads.at[k, span(c)], load_sem.at[side, c]
        )

    def stage_a(c):
        return remote(sent.at[span(c)], got_a.at[span(c)], sems.at[0, c], sems.at[1, c], mate)

    def stage_b(c):
        source = mid.at[span(c), theirs]
        return remote(source, got_b.at[span(c)], sems.at[2, c], sems.at[3, c], across)

    def stage_c(c, k):
        there = result.at[k, span(c)]
        return remote(there, there, sems.at[4, c], sems.at[5, c], mate)

    def product(k, c):
        return jnp.dot(
            grads[k, span(c)], coeff_ref[k], preferred_element_type=jnp.float32
        )

    def image(k, c):
        total[k] += lax.dot_general(
            hidden[k, span(c)],
            grads[k, span(c)],
            (((0,), (0,)), ((), ())),
            preferred_element_type=jnp.float32,
        )

    def loop(body):
        lax.fori_loop(0, chunks, lambda c, _: body(c), None)

    def begin(c):
        load(c, 0).start()
        load(c, 1).start()

    def across_chunk(c):
        stage_a(c).wait_recv()
        mid[span(c)] = (own[span(c)] + got_a[span(c)].astype(jnp.float32)).astype(mid.dtype)
        stage_b(c).start()

    def forward(c):
        load(c, 0).wait()
        sent[span(c)] = product(1 - low, c).astype(sent.dtype)
        stage_a(c).start()
        load(c, 1).wait()
        own[span(c)] = product(low, c)

        @pl.when(c > 0)
        def _():
            across_chunk(c - 1)

    def other(c):
        stage_c(c, 1 - low).wait_recv()
        if not scatter:
            image(1 - low, c)

    def backward(c):
        stage_b(c).wait_recv()
        result[low, span(c)] = (
            mid[span(c), mine].astype(jnp.float32) + got_b[span(c)].astype(jnp.float32)
        ).astype(result.dtype)
        stage_c(c, low).start()
        if not scatter:
            image(low, c)

        @pl.when(c > 0)
        def _():
            other(c - 1)

    def finish(c):
        stage_a(c).wait_send()
        stage_b(c).wait_send()
        stage_c(c, low).wait_send()

    loop(begin)
    if not scatter:
        total[...] = jnp.zeros_like(total)
    greet([mate, across])
    loop(forward)
    across_chunk(chunks - 1)
    loop(backward)
    other(chunks - 1)
    if not scatter:
        out_ref[...] = total[...].astype(out_ref.dtype)
    loop(finish)


def hidden_sums(out_grads, coeff, chunks, scatter, collective_id):
    parts, units, tokens = out_grads.shape
    rank = coeff.shape[2]
    width = rank // 2 if scatter else rank
    half = jnp.bfloat16
    return pl.pallas_call(
        functools.partial(hidden_kernel, chunks, scatter),
        out_shape=jax.ShapeDtypeStruct(
            (parts, units, width) if scatter else (parts, rank, tokens), half
        ),
        in_specs=[
            pl.BlockSpec(memory_space=pl.ANY),
            pl.BlockSpec(memory_space=pltpu.VMEM),
        ],
        out_specs=pl.BlockSpec(memory_space=pltpu.VMEM),
        scratch_shapes=[
            pltpu.VMEM(out_grads.shape, half),
            pltpu.VMEM((units, rank), half),
            pltpu.VMEM((units, rank), jnp.float32),
            pltpu.VMEM((units, rank), half),
            pltpu.VMEM((units, rank), half),
            pltpu.VMEM((units, width), half),
            pltpu.VMEM((8, 128) if scatter else (parts, units, rank), half),
            pltpu.VMEM((8, 128) if scatter else (parts, rank, tokens), jnp.float32),
            pltpu.SemaphoreType.DMA((2, chunks)),
            pltpu.SemaphoreType.DMA((6, chunks)),
        ],
        compiler_params=pltpu.CompilerParams(
            collective_id=collective_id, has_side_effects=True, vmem_limit_bytes=VMEM_LIMIT
        ),
        name="hidden_sums",
    )(out_grads, coeff)


def eliminate(blocks):
    shape = (BLOCK // 8, 8, 2 * BLOCK)
    index = lax.broadcasted_iota(jnp.int32, shape, 0) * 8 + lax.broadcasted_iota(
        jnp.int32, shape, 1
    )
    wide = (8, 2 * BLOCK)
    blocks = [block.reshape(shape) for block in blocks]
    scales = [jnp.zeros(shape, jnp.float32) for _ in blocks]
    for j in range(0, BLOCK, GROUP):
        for k, block in enumerate(blocks):
            rows, columns, cross = [], [], []
            for q in range(GROUP):
                line = block[(j + q) // 8, (j + q) % 8 : (j + q) % 8 + 1, :]
                rows.append(jnp.broadcast_to(line, wide))
                columns.append(jnp.broadcast_to(block[:, :, j + q : j + q + 1], shape))
                cross.append(
                    [jnp.broadcast_to(line[:, j + s : j + s + 1], wide) for s in range(GROUP)]
                )
            for q in range(GROUP):
                pivot = cross[q][q]
                reciprocal = 1.0 / pivot
                for s in range(q + 1, GROUP):
                    ratio = cross[q][s] * reciprocal
                    for u in range(s, GROUP):
                        cross[s][u] = cross[s][u] - ratio * cross[q][u]
                    rows[s] = rows[s] - ratio * rows[q]
                    columns[s] = columns[s] - ratio[None] * columns[q]
                factor = jnp.where(index > j + q, columns[q], 0.0)
                block = block - factor * (rows[q] * reciprocal)[None]
                scales[k] = jnp.where(index == j + q, lax.rsqrt(pivot)[None], scales[k])
            blocks[k] = block
    return [
        (block * scale).reshape(BLOCK, 2 * BLOCK)[:, BLOCK:]
        for block, scale in zip(blocks, scales)
    ]


def inverse_factor(out_ref, work):
    parts, size, _ = out_ref.shape
    exact = functools.partial(
        lax.dot_general, precision=lax.Precision.HIGHEST, preferred_element_type=jnp.float32
    )
    row = lax.broadcasted_iota(jnp.int32, (size, size), 0)
    column = lax.broadcasted_iota(jnp.int32, (size, size), 1)
    for k in range(parts):
        work[k, :, size:] = jnp.where(row == column, 1.0, 0.0)
    small = jnp.where(row == column, 1.0, 0.0)[:BLOCK, :BLOCK]
    for start in range(0, size, BLOCK):
        stop = start + BLOCK
        inverses = eliminate(
            [
                jnp.concatenate([work[k, start:stop, start:stop], small], axis=1)
                for k in range(parts)
            ]
        )
        for k, inverse in enumerate(inverses):
            done = exact(inverse, work[k, start:stop, :], (((1,), (0,)), ((), ())))
            out_ref[k, start:stop, :] = done[:, size:]
            if stop < size:
                below = exact(work[k, stop:, start:stop], inverse, (((1,), (1,)), ((), ())))
                work[k, stop:, :] -= exact(below, done, (((1,), (0,)), ((), ())))


def settle_kernel(
    n, gram_ref, local_ref, coeff_ref, inverse_ref, got_g, got_c, full, work, sem_g, sem_c, sem_m
):
    me, quarter = lax.axis_index("dp"), lax.axis_index("mp")
    parts, size, _ = inverse_ref.shape
    peers = [{"dp": lax.rem(me + step, n)} for step in range(1, n)]
    beside = [{"mp": lax.rem(quarter + step, 4)} for step in range(1, 4)]
    greet(peers + beside)
    started = []

    def send(*copy):
        started.append(remote(*copy))
        started[-1].start()

    for i, peer in enumerate(peers):
        send(gram_ref.at[quarter, peer["dp"]], got_g.at[i], sem_g.at[0, i], sem_g.at[1, i], peer)
    total = gram_ref[quarter, me]
    for i, peer in enumerate(peers):
        remote(got_g.at[i], got_g.at[i], sem_g.at[0, i], sem_g.at[1, i], peer).wait_recv()
        total = total + got_g[i]
    full[quarter, me] = total
    own = full.at[quarter, me]
    for i, peer in enumerate(peers):
        send(own, own, sem_g.at[2, i], sem_g.at[3, i], peer)
    for i, peer in enumerate(peers):
        landed = full.at[quarter, lax.rem(me + n - 1 - i, n)]
        remote(landed, landed, sem_g.at[2, i], sem_g.at[3, i], peer).wait_recv()
    for i, peer in enumerate(beside):
        send(full.at[quarter], full.at[quarter], sem_m.at[0, i], sem_m.at[1, i], peer)
    for i, peer in enumerate(beside):
        landed = full.at[lax.rem(quarter + 3 - i, 4)]
        remote(landed, landed, sem_m.at[0, i], sem_m.at[1, i], peer).wait_recv()
    for i, peer in enumerate(peers):
        send(local_ref.at[peer["dp"]], got_c.at[i], sem_c.at[0, i], sem_c.at[1, i], peer)
    for k in range(parts):
        work[k, :, :size] = full[2 * k : 2 * k + 2].reshape(size, size)
    inverse_factor(inverse_ref, work)
    total = local_ref[me]
    for i, peer in enumerate(peers):
        remote(got_c.at[i], got_c.at[i], sem_c.at[0, i], sem_c.at[1, i], peer).wait_recv()
        total = total + got_c[i]
    coeff_ref[me] = lax.dot_general(
        total,
        inverse_ref[me // (n // parts)],
        (((1,), (1,)), ((), ())),
        precision=lax.Precision.HIGHEST,
        preferred_element_type=jnp.float32,
    ).astype(coeff_ref.dtype)
    own = coeff_ref.at[me]
    for i, peer in enumerate(peers):
        send(own, own, sem_c.at[2, i], sem_c.at[3, i], peer)
    for i, peer in enumerate(peers):
        landed = coeff_ref.at[lax.rem(me + n - 1 - i, n)]
        remote(landed, landed, sem_c.at[2, i], sem_c.at[3, i], peer).wait_recv()
    for copy in started:
        copy.wait_send()


def settle(n, gram, local, collective_id):
    parts, size, _ = gram.shape
    rows, columns = local.shape
    piece, share = rows // n, parts * size // (4 * n)
    coeff, inverse = pl.pallas_call(
        functools.partial(settle_kernel, n),
        out_shape=(
            jax.ShapeDtypeStruct((n, piece, columns), jnp.bfloat16),
            jax.ShapeDtypeStruct(gram.shape, jnp.float32),
        ),
        in_specs=[pl.BlockSpec(memory_space=pltpu.VMEM)] * 2,
        out_specs=[pl.BlockSpec(memory_space=pltpu.VMEM)] * 2,
        scratch_shapes=[
            pltpu.VMEM((n - 1, share, size), jnp.float32),
            pltpu.VMEM((n - 1, piece, columns), jnp.float32),
            pltpu.VMEM((4, n, share, size), jnp.float32),
            pltpu.VMEM((parts, size, 2 * size), jnp.float32),
            pltpu.SemaphoreType.DMA((4, n - 1)),
            pltpu.SemaphoreType.DMA((4, n - 1)),
            pltpu.SemaphoreType.DMA((2, 3)),
        ],
        compiler_params=pltpu.CompilerParams(
            collective_id=collective_id, has_side_effects=True, vmem_limit_bytes=VMEM_LIMIT
        ),
        name="settle",
    )(gram.reshape(4, n, share, size), local.reshape(n, piece, columns))
    return coeff.reshape(rows, columns), inverse


def shards(dp, acts, out_grads, proj_old, moment_one, moment_two):
    half = jnp.bfloat16
    parts, units, tokens = out_grads.shape
    features, rank = proj_old.shape[1:]
    einsum = functools.partial(jnp.einsum, preferred_element_type=jnp.float32)

    def feature_product(basis_half):
        return einsum("dt,kdr->ktr", acts, basis_half).reshape(parts * tokens, rank)

    def sweep(_, carried):
        coeff = carried[0].reshape(parts, tokens, rank)
        token_part = hidden_sums(out_grads, coeff, 14, False, 1)
        token_image = reduce_dp(dp, token_part.reshape(parts * rank, tokens), 5)
        image_part = einsum("dt,krt->kdr", acts, token_image.reshape(parts, rank, tokens))
        image = reduce_mp(image_part.astype(half).reshape(parts * features, rank), 4, 2)
        image = image.reshape(parts, features, rank)
        coeff, inverse = settle(
            dp, einsum("kdr,kds->krs", image, image), feature_product(image), 3
        )
        return coeff, image, inverse

    coeff = reduce_dp(dp, feature_product(proj_old.astype(half)).astype(half), 0)
    empty = jnp.zeros((parts, features, rank), half), jnp.zeros((parts, rank, rank), jnp.float32)
    coeff, image, inverse = lax.fori_loop(0, SWEEPS, sweep, (coeff, *empty))
    basis = jnp.einsum(
        "kdr,ksr->kds", image.astype(jnp.float32), inverse, precision=lax.Precision.HIGHEST
    )
    projected = hidden_sums(out_grads, coeff.reshape(parts, tokens, rank), 14, True, 4)
    share = rank // 4
    low = lax.rem(lax.axis_index("mp"), 2)
    projected = lax.dynamic_slice_in_dim(projected, low * share, share, 2)
    projected = projected.astype(jnp.float32)
    first_new = 0.9 * moment_one + 0.1 * projected
    second_new = 0.999 * moment_two + 0.001 * projected * projected
    step_update = first_new / (jnp.sqrt(second_new) + 1e-08)
    return (basis, first_new, second_new, step_update)


def solution(mesh):
    assert mesh.shape["mp"] == 4
    placed = (
        P("dp", "mp"),
        P(None, "dp", "mp"),
        P(None, "dp", None),
        P(None, "dp", "mp"),
        P(None, "dp", "mp"),
    )
    return jax.shard_map(
        functools.partial(shards, mesh.shape["dp"]),
        mesh=mesh,
        in_specs=placed,
        out_specs=(
            P(None, "dp", None),
            P(None, "dp", "mp"),
            P(None, "dp", "mp"),
            P(None, "dp", "mp"),
        ),
        check_vma=False,
    )
```

```python
import functools

import jax
import jax.numpy as jnp
from jax import lax
from jax.experimental import pallas as pl
from jax.experimental.pallas import tpu as pltpu
from jax.sharding import PartitionSpec as P

SWEEPS = 2
BLOCK = 64
GROUP = 4
VMEM_LIMIT = 48 << 20


def greet(peers):
    barrier = pltpu.get_barrier_semaphore()
    for peer in peers:
        pl.semaphore_signal(barrier, inc=1, device_id=peer, device_id_type=pl.DeviceIdType.MESH)
    pl.semaphore_wait(barrier, len(peers))


def remote(src, dst, send_sem, recv_sem, peer):
    return pltpu.make_async_remote_copy(
        src_ref=src,
        dst_ref=dst,
        send_sem=send_sem,
        recv_sem=recv_sem,
        device_id=peer,
        device_id_type=pl.DeviceIdType.MESH,
    )


def reduce_dp_kernel(n, x_ref, out_ref, got, send_a, recv_a, send_b, recv_b):
    me = lax.axis_index("dp")
    peers = [lax.rem(me + step, n) for step in range(1, n)]
    greet([{"dp": peer} for peer in peers])
    first = []
    for i, peer in enumerate(peers):
        copy = remote(x_ref.at[peer], got.at[i], send_a.at[i], recv_a.at[i], {"dp": peer})
        copy.start()
        first.append(copy)
    total = x_ref[me].astype(jnp.float32)
    for i, copy in enumerate(first):
        copy.wait_recv()
        total = total + got[i].astype(jnp.float32)
    out_ref[me] = total.astype(out_ref.dtype)
    second = []
    for i, peer in enumerate(peers):
        copy = remote(out_ref.at[me], out_ref.at[me], send_b.at[i], recv_b.at[i], {"dp": peer})
        copy.start()
        second.append(copy)
    for i, copy in enumerate(second):
        source = lax.rem(me + n - 1 - i, n)
        landed = out_ref.at[source]
        remote(landed, landed, send_b.at[i], recv_b.at[i], {"dp": peers[i]}).wait_recv()
    for copy in first + second:
        copy.wait_send()


def reduce_dp(n, x, collective_id):
    rows, columns = x.shape
    piece = rows // n
    out = pl.pallas_call(
        functools.partial(reduce_dp_kernel, n),
        out_shape=jax.ShapeDtypeStruct((n, piece, columns), x.dtype),
        in_specs=[pl.BlockSpec(memory_space=pltpu.VMEM)],
        out_specs=pl.BlockSpec(memory_space=pltpu.VMEM),
        scratch_shapes=[pltpu.VMEM((n - 1, piece, columns), x.dtype)]
        + [pltpu.SemaphoreType.DMA((n - 1,))] * 4,
        compiler_params=pltpu.CompilerParams(
            collective_id=collective_id, has_side_effects=True, vmem_limit_bytes=VMEM_LIMIT
        ),
        name="reduce_dp",
    )(x.reshape(n, piece, columns))
    return out.reshape(rows, columns)


def reduce_mp_kernel(chunks, x_ref, out_ref, got_a, mid, got_b, sems):
    me = lax.axis_index("mp")
    low, high = lax.rem(me, 2), me // 2
    mate = {"mp": high * 2 + 1 - low}
    across = {"mp": (1 - high) * 2 + low}
    rows = x_ref.shape[1]
    piece = rows // chunks
    greet([mate, across])
    stage_a, stage_b, stage_c = [], [], []
    for c in range(chunks):
        span = pl.ds(c * piece, piece)
        copy = remote(
            x_ref.at[1 - low, span], got_a.at[span], sems.at[0, c], sems.at[1, c], mate
        )
        copy.start()
        stage_a.append(copy)
    for c in range(chunks):
        span = pl.ds(c * piece, piece)
        stage_a[c].wait_recv()
        mid[span] = (
            x_ref[low, span].astype(jnp.float32) + got_a[span].astype(jnp.float32)
        ).astype(mid.dtype)
        copy = remote(mid.at[span], got_b.at[span], sems.at[2, c], sems.at[3, c], across)
        copy.start()
        stage_b.append(copy)
    for c in range(chunks):
        span = pl.ds(c * piece, piece)
        stage_b[c].wait_recv()
        out_ref[low, span] = (
            mid[span].astype(jnp.float32) + got_b[span].astype(jnp.float32)
        ).astype(out_ref.dtype)
        copy = remote(
            out_ref.at[low, span], out_ref.at[low, span], sems.at[4, c], sems.at[5, c], mate
        )
        copy.start()
        stage_c.append(copy)
    for c in range(chunks):
        landed = out_ref.at[1 - low, pl.ds(c * piece, piece)]
        remote(landed, landed, sems.at[4, c], sems.at[5, c], mate).wait_recv()
    for copy in stage_a + stage_b + stage_c:
        copy.wait_send()


def reduce_mp(x, chunks, collective_id):
    rows, columns = x.shape
    half = rows // 2
    out = pl.pallas_call(
        functools.partial(reduce_mp_kernel, chunks),
        out_shape=jax.ShapeDtypeStruct((2, half, columns), x.dtype),
        in_specs=[pl.BlockSpec(memory_space=pltpu.VMEM)],
        out_specs=pl.BlockSpec(memory_space=pltpu.VMEM),
        scratch_shapes=[
            pltpu.VMEM((half, columns), x.dtype),
            pltpu.VMEM((half, columns), x.dtype),
            pltpu.VMEM((half, columns), x.dtype),
            pltpu.SemaphoreType.DMA((6, chunks)),
        ],
        compiler_params=pltpu.CompilerParams(
            collective_id=collective_id, has_side_effects=True, vmem_limit_bytes=VMEM_LIMIT
        ),
        name="reduce_mp",
    )(x.reshape(2, half, columns))
    return out.reshape(rows, columns)


def hidden_kernel(
    chunks, scatter, grads_ref, coeff_ref, out_ref, grads, sent, own, got_a, mid, got_b, hidden,
    total, load_sem, sems
):
    me = lax.axis_index("mp")
    low, high = lax.rem(me, 2), me // 2
    mate = {"mp": high * 2 + 1 - low}
    across = {"mp": (1 - high) * 2 + low}
    parts, units, tokens = grads_ref.shape
    piece = units // chunks
    result = out_ref if scatter else hidden
    width = result.shape[2]
    mine = pl.ds(pl.multiple_of(high * width, 128), width) if scatter else slice(None)
    theirs = pl.ds(pl.multiple_of((1 - high) * width, 128), width) if scatter else slice(None)

    def span(c):
        return pl.ds(pl.multiple_of(c * piece, piece), piece)

    def load(c, side):
        k = 1 - low if side == 0 else low
        return pltpu.make_async_copy(
            grads_ref.at[k, span(c)], grads.at[k, span(c)], load_sem.at[side, c]
        )

    def stage_a(c):
        return remote(sent.at[span(c)], got_a.at[span(c)], sems.at[0, c], sems.at[1, c], mate)

    def stage_b(c):
        source = mid.at[span(c), theirs]
        return remote(source, got_b.at[span(c)], sems.at[2, c], sems.at[3, c], across)

    def stage_c(c, k):
        there = result.at[k, span(c)]
        return remote(there, there, sems.at[4, c], sems.at[5, c], mate)

    def product(k, c):
        return jnp.dot(
            grads[k, span(c)], coeff_ref[k], preferred_element_type=jnp.float32
        )

    def image(k, c):
        total[k] += lax.dot_general(
            hidden[k, span(c)],
            grads[k, span(c)],
            (((0,), (0,)), ((), ())),
            preferred_element_type=jnp.float32,
        )

    def loop(body):
        lax.fori_loop(0, chunks, lambda c, _: body(c), None)

    def begin(c):
        load(c, 0).start()
        load(c, 1).start()

    def across_chunk(c):
        stage_a(c).wait_recv()
        mid[span(c)] = (own[span(c)] + got_a[span(c)].astype(jnp.float32)).astype(mid.dtype)
        stage_b(c).start()

    def forward(c):
        load(c, 0).wait()
        sent[span(c)] = product(1 - low, c).astype(sent.dtype)
        stage_a(c).start()
        load(c, 1).wait()
        own[span(c)] = product(low, c)

        @pl.when(c > 0)
        def _():
            across_chunk(c - 1)

    def other(c):
        stage_c(c, 1 - low).wait_recv()
        if not scatter:
            image(1 - low, c)

    def backward(c):
        stage_b(c).wait_recv()
        result[low, span(c)] = (
            mid[span(c), mine].astype(jnp.float32) + got_b[span(c)].astype(jnp.float32)
        ).astype(result.dtype)
        stage_c(c, low).start()
        if not scatter:
            image(low, c)

        @pl.when(c > 0)
        def _():
            other(c - 1)

    def finish(c):
        stage_a(c).wait_send()
        stage_b(c).wait_send()
        stage_c(c, low).wait_send()

    loop(begin)
    if not scatter:
        total[...] = jnp.zeros_like(total)
    greet([mate, across])
    loop(forward)
    across_chunk(chunks - 1)
    loop(backward)
    other(chunks - 1)
    if not scatter:
        out_ref[...] = total[...].astype(out_ref.dtype)
    loop(finish)


def hidden_sums(out_grads, coeff, chunks, scatter, collective_id):
    parts, units, tokens = out_grads.shape
    rank = coeff.shape[2]
    width = rank // 2 if scatter else rank
    half = jnp.bfloat16
    return pl.pallas_call(
        functools.partial(hidden_kernel, chunks, scatter),
        out_shape=jax.ShapeDtypeStruct(
            (parts, units, width) if scatter else (parts, rank, tokens), half
        ),
        in_specs=[
            pl.BlockSpec(memory_space=pl.ANY),
            pl.BlockSpec(memory_space=pltpu.VMEM),
        ],
        out_specs=pl.BlockSpec(memory_space=pltpu.VMEM),
        scratch_shapes=[
            pltpu.VMEM(out_grads.shape, half),
            pltpu.VMEM((units, rank), half),
            pltpu.VMEM((units, rank), jnp.float32),
            pltpu.VMEM((units, rank), half),
            pltpu.VMEM((units, rank), half),
            pltpu.VMEM((units, width), half),
            pltpu.VMEM((8, 128) if scatter else (parts, units, rank), half),
            pltpu.VMEM((8, 128) if scatter else (parts, rank, tokens), jnp.float32),
            pltpu.SemaphoreType.DMA((2, chunks)),
            pltpu.SemaphoreType.DMA((6, chunks)),
        ],
        compiler_params=pltpu.CompilerParams(
            collective_id=collective_id, has_side_effects=True, vmem_limit_bytes=VMEM_LIMIT
        ),
        name="hidden_sums",
    )(out_grads, coeff)


def eliminate(blocks):
    shape = (BLOCK // 8, 8, 2 * BLOCK)
    index = lax.broadcasted_iota(jnp.int32, shape, 0) * 8 + lax.broadcasted_iota(
        jnp.int32, shape, 1
    )
    wide = (8, 2 * BLOCK)
    blocks = [block.reshape(shape) for block in blocks]
    scales = [jnp.zeros(shape, jnp.float32) for _ in blocks]
    for j in range(0, BLOCK, GROUP):
        for k, block in enumerate(blocks):
            rows, columns, cross = [], [], []
            for q in range(GROUP):
                line = block[(j + q) // 8, (j + q) % 8 : (j + q) % 8 + 1, :]
                rows.append(jnp.broadcast_to(line, wide))
                columns.append(jnp.broadcast_to(block[:, :, j + q : j + q + 1], shape))
                cross.append(
                    [jnp.broadcast_to(line[:, j + s : j + s + 1], wide) for s in range(GROUP)]
                )
            for q in range(GROUP):
                pivot = cross[q][q]
                reciprocal = 1.0 / pivot
                for s in range(q + 1, GROUP):
                    ratio = cross[q][s] * reciprocal
                    for u in range(s, GROUP):
                        cross[s][u] = cross[s][u] - ratio * cross[q][u]
                    rows[s] = rows[s] - ratio * rows[q]
                    columns[s] = columns[s] - ratio[None] * columns[q]
                factor = jnp.where(index > j + q, columns[q], 0.0)
                block = block - factor * (rows[q] * reciprocal)[None]
                scales[k] = jnp.where(index == j + q, lax.rsqrt(pivot)[None], scales[k])
            blocks[k] = block
    return [
        (block * scale).reshape(BLOCK, 2 * BLOCK)[:, BLOCK:]
        for block, scale in zip(blocks, scales)
    ]


def inverse_factor(out_ref, work):
    parts, size, _ = out_ref.shape
    exact = functools.partial(
        lax.dot_general, precision=lax.Precision.HIGHEST, preferred_element_type=jnp.float32
    )
    row = lax.broadcasted_iota(jnp.int32, (size, size), 0)
    column = lax.broadcasted_iota(jnp.int32, (size, size), 1)
    for k in range(parts):
        work[k, :, size:] = jnp.where(row == column, 1.0, 0.0)
    small = jnp.where(row == column, 1.0, 0.0)[:BLOCK, :BLOCK]
    for start in range(0, size, BLOCK):
        stop = start + BLOCK
        inverses = eliminate(
            [
                jnp.concatenate([work[k, start:stop, start:stop], small], axis=1)
                for k in range(parts)
            ]
        )
        for k, inverse in enumerate(inverses):
            done = exact(inverse, work[k, start:stop, :], (((1,), (0,)), ((), ())))
            out_ref[k, start:stop, :] = done[:, size:]
            if stop < size:
                below = exact(work[k, stop:, start:stop], inverse, (((1,), (1,)), ((), ())))
                work[k, stop:, :] -= exact(below, done, (((1,), (0,)), ((), ())))


def settle_kernel(
    n, gram_ref, local_ref, coeff_ref, inverse_ref, got_g, got_c, full, work, sem_g, sem_c, sem_m
):
    me, quarter = lax.axis_index("dp"), lax.axis_index("mp")
    parts, size, _ = inverse_ref.shape
    peers = [{"dp": lax.rem(me + step, n)} for step in range(1, n)]
    beside = [{"mp": lax.rem(quarter + step, 4)} for step in range(1, 4)]
    greet(peers + beside)
    started = []

    def send(*copy):
        started.append(remote(*copy))
        started[-1].start()

    for i, peer in enumerate(peers):
        send(gram_ref.at[quarter, peer["dp"]], got_g.at[i], sem_g.at[0, i], sem_g.at[1, i], peer)
    total = gram_ref[quarter, me]
    for i, peer in enumerate(peers):
        remote(got_g.at[i], got_g.at[i], sem_g.at[0, i], sem_g.at[1, i], peer).wait_recv()
        total = total + got_g[i]
    full[quarter, me] = total
    own = full.at[quarter, me]
    for i, peer in enumerate(peers):
        send(own, own, sem_g.at[2, i], sem_g.at[3, i], peer)
    for i, peer in enumerate(peers):
        landed = full.at[quarter, lax.rem(me + n - 1 - i, n)]
        remote(landed, landed, sem_g.at[2, i], sem_g.at[3, i], peer).wait_recv()
    for i, peer in enumerate(beside):
        send(full.at[quarter], full.at[quarter], sem_m.at[0, i], sem_m.at[1, i], peer)
    for i, peer in enumerate(beside):
        landed = full.at[lax.rem(quarter + 3 - i, 4)]
        remote(landed, landed, sem_m.at[0, i], sem_m.at[1, i], peer).wait_recv()
    for i, peer in enumerate(peers):
        send(local_ref.at[peer["dp"]], got_c.at[i], sem_c.at[0, i], sem_c.at[1, i], peer)
    for k in range(parts):
        work[k, :, :size] = full[2 * k : 2 * k + 2].reshape(size, size)
    inverse_factor(inverse_ref, work)
    total = local_ref[me]
    for i, peer in enumerate(peers):
        remote(got_c.at[i], got_c.at[i], sem_c.at[0, i], sem_c.at[1, i], peer).wait_recv()
        total = total + got_c[i]
    coeff_ref[me] = lax.dot_general(
        total,
        inverse_ref[me // (n // parts)],
        (((1,), (1,)), ((), ())),
        precision=lax.Precision.HIGHEST,
        preferred_element_type=jnp.float32,
    ).astype(coeff_ref.dtype)
    own = coeff_ref.at[me]
    for i, peer in enumerate(peers):
        send(own, own, sem_c.at[2, i], sem_c.at[3, i], peer)
    for i, peer in enumerate(peers):
        landed = coeff_ref.at[lax.rem(me + n - 1 - i, n)]
        remote(landed, landed, sem_c.at[2, i], sem_c.at[3, i], peer).wait_recv()
    for copy in started:
        copy.wait_send()


def settle(n, gram, local, collective_id):
    parts, size, _ = gram.shape
    rows, columns = local.shape
    piece, share = rows // n, parts * size // (4 * n)
    coeff, inverse = pl.pallas_call(
        functools.partial(settle_kernel, n),
        out_shape=(
            jax.ShapeDtypeStruct((n, piece, columns), jnp.bfloat16),
            jax.ShapeDtypeStruct(gram.shape, jnp.float32),
        ),
        in_specs=[pl.BlockSpec(memory_space=pltpu.VMEM)] * 2,
        out_specs=[pl.BlockSpec(memory_space=pltpu.VMEM)] * 2,
        scratch_shapes=[
            pltpu.VMEM((n - 1, share, size), jnp.float32),
            pltpu.VMEM((n - 1, piece, columns), jnp.float32),
            pltpu.VMEM((4, n, share, size), jnp.float32),
            pltpu.VMEM((parts, size, 2 * size), jnp.float32),
            pltpu.SemaphoreType.DMA((4, n - 1)),
            pltpu.SemaphoreType.DMA((4, n - 1)),
            pltpu.SemaphoreType.DMA((2, 3)),
        ],
        compiler_params=pltpu.CompilerParams(
            collective_id=collective_id, has_side_effects=True, vmem_limit_bytes=VMEM_LIMIT
        ),
        name="settle",
    )(gram.reshape(4, n, share, size), local.reshape(n, piece, columns))
    return coeff.reshape(rows, columns), inverse


def shards(dp, acts, out_grads, proj_old, moment_one, moment_two):
    half = jnp.bfloat16
    parts, units, tokens = out_grads.shape
    features, rank = proj_old.shape[1:]
    einsum = functools.partial(jnp.einsum, preferred_element_type=jnp.float32)

    def feature_product(basis_half):
        return einsum("dt,kdr->ktr", acts, basis_half).reshape(parts * tokens, rank)

    def sweep(_, carried):
        coeff = carried[0].reshape(parts, tokens, rank)
        token_part = hidden_sums(out_grads, coeff, 14, False, 1)
        token_image = reduce_dp(dp, token_part.reshape(parts * rank, tokens), 5)
        image_part = einsum("dt,krt->kdr", acts, token_image.reshape(parts, rank, tokens))
        image = reduce_mp(image_part.astype(half).reshape(parts * features, rank), 4, 2)
        image = image.reshape(parts, features, rank)
        coeff, inverse = settle(
            dp, einsum("kdr,kds->krs", image, image), feature_product(image), 3
        )
        return coeff, image, inverse

    coeff = reduce_dp(dp, feature_product(proj_old.astype(half)).astype(half), 0)
    empty = jnp.zeros((parts, features, rank), half), jnp.zeros((parts, rank, rank), jnp.float32)
    coeff, image, inverse = lax.fori_loop(0, SWEEPS, sweep, (coeff, *empty))
    basis = jnp.einsum(
        "kdr,ksr->kds", image.astype(jnp.float32), inverse, precision=lax.Precision.HIGHEST
    )
    projected = hidden_sums(out_grads, coeff.reshape(parts, tokens, rank), 14, True, 4)
    projected = projected.reshape(parts * units, rank // 2)
    share = rank // 4
    low = lax.rem(lax.axis_index("mp"), 2)
    projected = lax.dynamic_slice_in_dim(projected, low * share, share, 1)
    projected = projected.reshape(parts, units, share).astype(jnp.float32)
    first_new = 0.9 * moment_one + 0.1 * projected
    second_new = 0.999 * moment_two + 0.001 * projected * projected
    step_update = first_new / (jnp.sqrt(second_new) + 1e-08)
    return (basis, first_new, second_new, step_update)


def solution(mesh):
    assert mesh.shape["mp"] == 4
    placed = (
        P("dp", "mp"),
        P(None, "dp", "mp"),
        P(None, "dp", None),
        P(None, "dp", "mp"),
        P(None, "dp", "mp"),
    )
    return jax.shard_map(
        functools.partial(shards, mesh.shape["dp"]),
        mesh=mesh,
        in_specs=placed,
        out_specs=(
            P(None, "dp", None),
            P(None, "dp", "mp"),
            P(None, "dp", "mp"),
            P(None, "dp", "mp"),
        ),
        check_vma=False,
    )
```
